32 devices in a mesh: groups: 2 (over x), tm: 4 (over y, core), tile: 4 (over z).
Axes of the slice: x: 2, y: 2, z: 4, core: 2. Of those that a mesh axis runs over, the one named last changes fastest.
Arguments:
- activations: float32 [24, 8, 64, 384], P(('groups', 'tm'), 'tile'), parts along dimension 0, may hold values from -200 to 200, as said below
- gain_attention: float32 [384], replicated, may hold values from 0.1 to 1.9
- w_query: float32 [384, 384], replicated, may hold values from -10 to 10, as said below
- w_key: float32 [384, 384], replicated, may hold values from -10 to 10, as said below
- w_value: float32 [384, 384], replicated, may hold values from -0.3125 to 0.3125
- w_out: float32 [384, 384], replicated, may hold values from -0.3125 to 0.3125
- gain_conv: float32 [384], replicated, may hold values from 0.1 to 1.9
- conv_weight: float32 [27, 384, 384], P(None, 'tm'), may hold values from -0.0625 to 0.0625
Outputs:
- attended: float32 [24, 8, 64, 384], P(('groups', 'tm'), 'tile'), parts along dimension 0
- conv_out: float32 [24, 8, 64, 384], P(('groups', 'tm'), 'tile'), parts along dimension 0
The draws below stay inside these ranges and needn't reach their ends.
There are 2 independent parts, one for each index of `groups`. The reference program is written for one: setup_inputs(seed, part) draws one part's arguments, and reference() takes and returns one part's arrays. A program takes and returns all parts, laid end to end along the dimension named above; an argument that names none is the same for every part. Nothing has to cross between parts.
Inputs may be any that keep to these rules, and one draw needn't show every extreme that they name: `activations`: finite latent features. `w_query`: finite projection entries. `w_key`: finite projection entries.
All inputs are finite; a program needn't handle non-finite values.
Results may differ from the reference program's by a relative error of at most 0.00023.
Values sent between devices are 32-bit elements; how exact they have to be, the bound alone decides.
A program may use at most 128 MiB of HBM per device.

```python
import math
import jax
import jax.numpy as jnp
from jax import lax

C = 384
W = 64
FRAMES = 12
HEIGHT = 8


def draw_activations(key, part):
    base_key = jax.random.fold_in(key, 101)
    row_key = jax.random.fold_in(key, 102)
    column_key = jax.random.fold_in(key, 103)
    shape = (FRAMES, HEIGHT, W, C)
    row_scale = jnp.exp(jax.random.uniform(row_key, (FRAMES, HEIGHT, W, 1), jnp.float32, 0.0, math.log(10.0)))
    column_scale = jnp.exp(jax.random.uniform(column_key, (C,), jnp.float32, 0.0, math.log(10.0)))
    base = jnp.clip(jax.random.normal(base_key, shape, jnp.float32), -6.0, 6.0)
    values = base * row_scale * column_scale / 10.0
    return values.astype(jnp.float32)


def draw_w_query(key, part):
    base = jnp.clip(jax.random.normal(jax.random.fold_in(key, 201), (C, C), jnp.float32), -6.0, 6.0)
    return (2.5 * base / math.sqrt(C)).astype(jnp.float32)


def draw_w_key(key, part):
    base = jnp.clip(jax.random.normal(jax.random.fold_in(key, 203), (C, C), jnp.float32), -6.0, 6.0)
    return (base / math.sqrt(C)).astype(jnp.float32)


def block_scale(rng, shape, split, low, top_value):
    level, own = 1.0, jax.random.fold_in(rng, 6)
    for dim, blocks in split:
        heights = jnp.exp(jax.random.uniform(jax.random.fold_in(own, dim), (blocks,), jnp.float32, low / len(split), top_value / len(split)))
        level = level * jnp.repeat(heights, shape[dim] // blocks).reshape([-1 if axis == dim else 1 for axis in range(len(shape))])
    return level


def gaussian(rng, shape, width, bound, pieces=(), kind=jnp.bfloat16):
    level = block_scale(rng, shape, pieces, -0.22, 0.18) if pieces else 1.0
    drawn = jax.random.normal(rng, shape, jnp.float32) * width * level
    return jnp.minimum(jnp.maximum(drawn, -bound), bound).astype(kind)


def setup_inputs(seed: int = 0, part: int = 0) -> dict:
    keys = jax.random.split(jax.random.key(seed), 9)
    own_keys = jax.random.split(jax.random.fold_in(keys[8], part), 9)
    activations = draw_activations(jax.random.fold_in(jax.random.fold_in(keys[8], part), 71), part)
    gain_attention = jnp.clip(1.0 + 0.18 * jax.random.normal(keys[1], (C,), jnp.float32), 0.1, 1.9)
    w_query = draw_w_query(jax.random.fold_in(keys[8], 71), part)
    w_key = draw_w_key(jax.random.fold_in(keys[8], 71), part)
    w_value = gaussian(keys[4], (C, C), C ** -0.5, 0.3125, (), jnp.float32)
    w_out = gaussian(keys[5], (C, C), C ** -0.5, 0.3125, (), jnp.float32)
    gain_conv = jnp.clip(1.0 + 0.18 * jax.random.normal(keys[6], (C,), jnp.float32), 0.1, 1.9)
    conv_weight = gaussian(keys[7], (27, C, C), (27 * C) ** -0.5, 0.0625, ((1, 4),), jnp.float32)
    return dict(activations=activations, gain_attention=gain_attention, w_query=w_query, w_key=w_key, w_value=w_value, w_out=w_out, gain_conv=gain_conv, conv_weight=conv_weight)


def rms_scale(values, gain):
    return values * lax.rsqrt(lax.optimization_barrier(jnp.mean(values * values, axis=-1, keepdims=True)) + 1e-06) * gain

def reference(activations, gain_attention, w_query, w_key, w_value, w_out, gain_conv, conv_weight):
    highest = lax.Precision.HIGHEST
    frame_count, height_cells, width_cells, channels = activations.shape
    normed = rms_scale(activations, gain_attention).reshape(frame_count, height_cells * width_cells, channels)
    queries = jnp.einsum('fpc,cd->fpd', normed, w_query, precision=highest)
    key_rows = jnp.einsum('fpc,cd->fpd', normed, w_key, precision=highest)
    values = jnp.einsum('fpc,cd->fpd', normed, w_value, precision=highest)
    scale = 1.0 / jnp.sqrt(jnp.float32(channels))

    def one_frame(triple):
        query_frame, key_frame, value_frame = triple
        scores = jnp.dot(query_frame, key_frame.T, precision=highest) * scale
        weights = jax.nn.softmax(scores, axis=-1)
        return jnp.dot(weights, value_frame, precision=highest)
    mixed = lax.map(one_frame, (queries, key_rows, values))
    attended = activations + jnp.einsum('fpc,cd->fpd', mixed, w_out, precision=highest).reshape(activations.shape)
    hidden = jax.nn.silu(rms_scale(attended, gain_conv))
    padded = jnp.pad(hidden, ((2, 0), (1, 1), (1, 1), (0, 0)))
    conv_out = jnp.zeros(activations.shape, jnp.float32)
    for shift_t in range(3):
        for shift_y in range(3):
            for shift_x in range(3):
                window = padded[shift_t:shift_t + frame_count, shift_y:shift_y + height_cells, shift_x:shift_x + width_cells]
                conv_out = conv_out + jnp.einsum('thwc,cd->thwd', window, conv_weight[9 * shift_t + 3 * shift_y + shift_x], precision=highest)
    return (attended, conv_out)
```

```python
import functools
import math

import jax
import jax.numpy as jnp
from jax import lax
from jax.experimental import pallas as pl
from jax.experimental.pallas import tpu as pltpu
from jax.sharding import PartitionSpec as P

F32, BF16 = jnp.float32, jnp.bfloat16
VMEM_LIMIT = 56 * 1024 * 1024
CHUNKS = 3


def split(x):
    high = x.astype(BF16)
    return high, (x - high.astype(F32)).astype(BF16)


def dot3(a, b, dims=(((1,), (0,)), ((), ()))):
    dot = functools.partial(lax.dot_general, dimension_numbers=dims, preferred_element_type=F32)
    (ah, al), (bh, bl) = a, b
    return dot(ah, bh) + (dot(ah, bl) + dot(al, bh))


TRANSPOSED = (((1,), (1,)), ((), ()))


def rms(v, gain):
    return v * lax.rsqrt(jnp.mean(v * v, axis=-1, keepdims=True) + 1e-06) * gain


def attention_kernel(slots, position, own, *refs):
    lefts, rights = refs[:slots], refs[slots : 2 * slots]
    gain_a, wq, wk, wv, wo, gain_c, attended, hidden = refs[2 * slots :]
    me = position[0]
    gain = gain_a[...]
    x = own[...]
    normed = split(rms(x, gain))
    queries = dot3(normed, split(wq[...]))
    folded = split(dot3(split(queries), split(wk[...]), TRANSPOSED))
    scale = 1.0 / math.sqrt(x.shape[-1])
    cells = [normed]
    for s in range(1, slots + 1):
        block = jnp.where(me >= s, lefts[s - 1][...], rights[slots - s][...])
        cells.append(split(rms(block, gain)))
    keys = tuple(jnp.concatenate([c[i] for c in cells], axis=0) for i in range(2))
    scores = dot3(folded, keys, TRANSPOSED) * scale
    powers = jnp.exp(scores - jnp.max(scores, axis=-1, keepdims=True))
    summed = jnp.sum(powers, axis=-1, keepdims=True)
    gathered = dot3(split(powers), keys) / summed
    mixed = dot3(split(gathered), split(wv[...]))
    result = x + dot3(split(mixed), split(wo[...]))
    attended[...] = result
    v = rms(result, gain_c[...])
    hidden[...] = v / (1.0 + jnp.exp(-v))


def attention(position, own, lefts, rights, gain_a, wq, wk, wv, wo, gain_c):
    frames, tokens, channels = own.shape
    block = pl.BlockSpec((None, tokens, channels), lambda f, p: (f, 0, 0))
    gain = pl.BlockSpec((1, channels), lambda f, p: (0, 0))
    weight = pl.BlockSpec((channels, channels), lambda f, p: (0, 0))
    slots = len(lefts)
    shape = jax.ShapeDtypeStruct(own.shape, F32)
    return pl.pallas_call(
        functools.partial(attention_kernel, slots),
        grid_spec=pltpu.PrefetchScalarGridSpec(
            num_scalar_prefetch=1,
            grid=(frames,),
            in_specs=[block] * (1 + 2 * slots) + [gain] + [weight] * 4 + [gain],
            out_specs=[block, block],
        ),
        out_shape=[shape, shape],
        cost_estimate=pl.CostEstimate(flops=3 * 10**9, bytes_accessed=10**7, transcendentals=10**6),
        compiler_params=pltpu.CompilerParams(vmem_limit_bytes=VMEM_LIMIT),
    )(position, own, *lefts, *rights, gain_a.reshape(1, -1), wq, wk, wv, wo, gain_c.reshape(1, -1))


def conv_kernel(sizes, offsets, hidden, up, down, past, past_up, past_down, *refs):
    slots = len(sizes)
    shards = [refs[c * slots : (c + 1) * slots] for c in range(CHUNKS)]
    out, xh, xl, stage, wh, wl = refs[CHUNKS * slots :]
    frames, rows, width, channels = hidden.shape
    step = pl.program_id(0)

    @pl.when(step == 0)
    def _():
        cell = lax.broadcasted_iota(jnp.int32, (width, channels), 0)
        for f in range(frames + 2):
            for r in range(rows + 2):
                upper, middle, lower, t = (past_up, past, past_down, f) if f < 2 else (up, hidden, down, f - 2)
                if r == 0:
                    value = upper[t, 0]
                elif r == rows + 1:
                    value = lower[t, 0]
                else:
                    value = middle[t, r - 1]
                before = jnp.where(cell == 0, 0.0, pltpu.roll(value, 1, 0))
                after = jnp.where(cell == width - 1, 0.0, pltpu.roll(value, width - 1, 0))
                for c, v in enumerate((before, value, after)):
                    high, low = split(v)
                    xh[f, r, :, c * channels : (c + 1) * channels] = high
                    xl[f, r, :, c * channels : (c + 1) * channels] = low
        out[...] = jnp.zeros_like(out)

    direct = all(s % 16 == 0 for s in sizes)
    for chunk in range(CHUNKS):

        @pl.when(step // 3 == chunk)
        def _(chunk=chunk):
            for slot, size in enumerate(sizes):
                unit = math.gcd(*sizes)
                for c in range(3):
                    row = pl.multiple_of(c * channels + offsets[slot], unit)
                    value = shards[chunk][slot][c]
                    if direct:
                        high, low = split(value)
                        wh[pl.ds(row, size)] = high
                        wl[pl.ds(row, size)] = low
                    else:
                        stage[pl.ds(row, size)] = value

    if not direct:
        high, low = split(stage[...])
        wh[...] = high
        wl[...] = low
    a, b = step // 3, step % 3
    pixels = frames * rows * width
    left = xh[pl.ds(a, frames), pl.ds(b, rows)].reshape(pixels, 3 * channels)
    left_low = xl[pl.ds(a, frames), pl.ds(b, rows)].reshape(pixels, 3 * channels)
    out[...] += dot3((left, left_low), (wh[...], wl[...]))


def conv(offsets, halo, shards):
    hidden = halo[0]
    frames, rows, width, channels = hidden.shape
    sizes = tuple(s.shape[1] for s in shards[0])
    pixels = frames * rows * width
    whole = [pl.BlockSpec(h.shape, lambda g, o: (0, 0, 0, 0)) for h in halo]
    parts = []
    for chunk in range(CHUNKS):
        for size in sizes:
            parts.append(
                pl.BlockSpec(
                    (3, size, channels),
                    lambda g, o, chunk=chunk: (jnp.clip(g - 3 * chunk, 0, 2), 0, 0),
                )
            )
    direct = all(s % 16 == 0 for s in sizes)
    return pl.pallas_call(
        functools.partial(conv_kernel, sizes),
        grid_spec=pltpu.PrefetchScalarGridSpec(
            num_scalar_prefetch=1,
            grid=(9,),
            in_specs=whole + parts,
            out_specs=pl.BlockSpec((pixels, channels), lambda g, o: (0, 0)),
            scratch_shapes=[
                pltpu.VMEM((frames + 2, rows + 2, width, 3 * channels), BF16),
                pltpu.VMEM((frames + 2, rows + 2, width, 3 * channels), BF16),
                pltpu.VMEM((8 if direct else 3 * channels, channels), F32),
                pltpu.VMEM((3 * channels, channels), BF16),
                pltpu.VMEM((3 * channels, channels), BF16),
            ],
        ),
        out_shape=jax.ShapeDtypeStruct((pixels, channels), F32),
        cost_estimate=pl.CostEstimate(flops=9 * 10**9, bytes_accessed=2 * 10**7, transcendentals=0),
        compiler_params=pltpu.CompilerParams(vmem_limit_bytes=VMEM_LIMIT),
    )(offsets, *halo, *[s for chunk in shards for s in chunk])


def exchange(x, axis, bit):
    return lax.ppermute(x, axis, [(i, i ^ bit) for i in range(lax.axis_size(axis))])


def kernel_shards(conv_weight):
    shards, groups = lax.axis_size("tm"), lax.axis_size("groups")
    me, group = lax.axis_index("tm"), lax.axis_index("groups")
    size = conv_weight.shape[1]
    taps = conv_weight.shape[0] // CHUNKS
    pieces = [conv_weight[c * taps : (c + 1) * taps] for c in range(CHUNKS)]
    halved = groups == 2 and size % 32 == 0
    half = size // 2
    chunks = []
    for piece in pieces:
        slots, offsets = [piece], [me * size]
        far = 1
        while 2 * far < shards:
            far *= 2
        held = [(0, 0, piece)]
        bit = far
        while bit >= 1:
            arrived = []
            for mask, kind, array in held:
                if halved and bit > 1 and kind == 0:
                    mine = lax.dynamic_slice_in_dim(array, group * half, half, axis=1)
                    first = exchange(mine, "tm", bit)
                    second = exchange(first, "groups", 1)
                    arrived += [(mask ^ bit, 1, first), (mask ^ bit, 2, second)]
                else:
                    arrived.append((mask ^ bit, kind, exchange(array, "tm", bit)))
            held += arrived
            bit //= 2
        chunks.append([array for _, _, array in held])
    starts = {0: 0, 1: group * half, 2: (1 - group) * half}
    offsets = jnp.stack([(me ^ mask) * size + starts[kind] for mask, kind, _ in held])
    return offsets.astype(jnp.int32), chunks


def line_gather(x, axis):
    size = lax.axis_size(axis)
    up = [(i, i + 1) for i in range(size - 1)]
    down = [(i + 1, i) for i in range(size - 1)]
    lefts, rights = [], []
    left = right = x
    for _ in range(size - 1):
        left = lax.ppermute(left, axis, up)
        right = lax.ppermute(right, axis, down)
        lefts.append(left)
        rights.append(right)
    return lefts, rights


def shifted(x, frame_step, tile_step):
    times, tiles = lax.axis_size("tm"), lax.axis_size("tile")
    route = []
    for t in range(times):
        for z in range(tiles):
            if t + frame_step < times and 0 <= z + tile_step < tiles:
                route.append((t * tiles + z, (t + frame_step) * tiles + z + tile_step))
    return lax.ppermute(x, ("tm", "tile"), route)


def body(activations, gain_attention, w_query, w_key, w_value, w_out, gain_conv, conv_weight):
    frames, rows, width, channels = activations.shape
    own = activations.reshape(frames, rows * width, channels)
    lefts, rights = line_gather(own, "tile")
    offsets, shards = kernel_shards(conv_weight)
    position = lax.axis_index("tile").reshape(1).astype(jnp.int32)
    attended, hidden = attention(
        position, own, lefts, rights, gain_attention, w_query, w_key, w_value, w_out, gain_conv
    )
    hidden = hidden.reshape(activations.shape)
    last = hidden[frames - 2 :]
    halo = (
        hidden,
        shifted(hidden[:, rows - 1 :], 0, 1),
        shifted(hidden[:, :1], 0, -1),
        shifted(last, 1, 0),
        shifted(last[:, rows - 1 :], 1, 1),
        shifted(last[:, :1], 1, -1),
    )
    conv_out = conv(offsets, halo, shards)
    return (attended.reshape(activations.shape), conv_out.reshape(activations.shape))


def solution(mesh):
    placed = P(("groups", "tm"), "tile", None, None)
    return jax.shard_map(
        body,
        mesh=mesh,
        in_specs=(placed, P(), P(), P(), P(), P(), P(), P(None, "tm", None)),
        out_specs=(placed, placed),
        check_vma=False,
    )
```

```python
import functools
import math

import jax
import jax.numpy as jnp
from jax import lax
from jax.experimental import pallas as pl
from jax.experimental.pallas import tpu as pltpu
from jax.sharding import PartitionSpec as P

F32, BF16 = jnp.float32, jnp.bfloat16
VMEM_LIMIT = 56 * 1024 * 1024
CHUNKS = 3


def split(x):
    high = x.astype(BF16)
    return high, (x - high.astype(F32)).astype(BF16)


def dot3(a, b, dims=(((1,), (0,)), ((), ()))):
    dot = functools.partial(lax.dot_general, dimension_numbers=dims, preferred_element_type=F32)
    (ah, al), (bh, bl) = a, b
    return dot(ah, bh) + (dot(ah, bl) + dot(al, bh))


TRANSPOSED = (((1,), (1,)), ((), ()))


def rms(v, gain):
    return v * lax.rsqrt(jnp.mean(v * v, axis=-1, keepdims=True) + 1e-06) * gain


MESH = pl.DeviceIdType.MESH


def shard_plan(shards, halved):
    plan, held = [], [(0, 0, None)]
    bit = 1
    while 2 * bit < shards:
        bit *= 2
    while bit >= 1 and shards > 1:
        arrived = []
        for mask, part, source in held:
            if halved and bit > 1 and part == 0:
                plan.append(("tm", bit, mask, 1, source))
                plan.append(("groups", 1, mask ^ bit, 1, len(plan) - 1))
                arrived += [(mask ^ bit, 1, len(plan) - 2), (mask ^ bit, 2, len(plan) - 1)]
            else:
                plan.append(("tm", bit, mask, part, source))
                arrived.append((mask ^ bit, part, len(plan) - 1))
        held += arrived
        bit //= 2
    return plan


def kernel(
    plan, times, tiles, act, gain_a, wq, wk, wv, wo, gain_c, kernel_hbm, attended, out,
    others, hid, up, down, past, past_up, past_down, weights, xh, xl,
    line_send, line_recv, edge_send, edge_recv, shard_send, shard_recv, own_sem,
):
    frames, rows, width, channels = hid.shape
    tokens = rows * width
    group, me, tile = lax.axis_index("groups"), lax.axis_index("tm"), lax.axis_index("tile")
    size = kernel_hbm.shape[1]
    half = size // 2

    barrier = pltpu.get_barrier_semaphore()
    friends = [(True, {"groups": 1 - group})]
    bit = 1
    while bit < times:
        friends.append((True, {"tm": me + bit * (1 - 2 * ((me // bit) % 2))}))
        bit *= 2
    for dt, dz in ((0, 1), (1, 0), (1, 1), (1, -1)):
        for sign in (1, -1):
            t, z = me + sign * dt, tile + sign * dz
            inside = (t >= 0) & (t < times) & (z >= 0) & (z < tiles)
            friends.append((inside, {"tm": t, "tile": z}))
    count = 0
    for inside, device in friends:
        if inside is True:
            pl.semaphore_signal(barrier, inc=1, device_id=device, device_id_type=MESH)
            count = count + 1
        else:

            @pl.when(inside)
            def _(device=device):
                pl.semaphore_signal(barrier, inc=1, device_id=device, device_id_type=MESH)

            count = count + inside.astype(jnp.int32)
    pl.semaphore_wait(barrier, count)

    def copy(src, dst, send, recv, device):
        return pltpu.make_async_remote_copy(
            src_ref=src, dst_ref=dst, send_sem=send, recv_sem=recv, device_id=device, device_id_type=MESH
        )

    def line(f, distance, direction):
        slot_here = distance - 1 if direction > 0 else tiles - distance + 1
        slot_there = distance if direction > 0 else tiles - distance
        src = act.at[f] if distance == 1 else others.at[f, slot_here - 1]
        side = 0 if direction > 0 else 1
        return copy(
            src, others.at[f, slot_there - 1], line_send.at[f, side, distance - 1],
            line_recv.at[f, slot_there - 1], {"tile": tile + direction},
        )

    def sends(distance, direction):
        if direction > 0:
            return (tile >= distance - 1) & (tile < tiles - 1)
        return (tile + distance - 1 <= tiles - 1) & (tile > 0)

    def flip(value, bit):
        return value + bit * (1 - 2 * ((value // bit) % 2))

    def flipped(mask):
        value, bit = me, 1
        while bit <= mask:
            if mask & bit:
                value = flip(value, bit)
            bit *= 2
        return value

    def region(ref, chunk, shard, part, swap, local=False):
        first = group if not swap else 1 - group
        start = {0: 0, 1: first * half, 2: (1 - first) * half}[part]
        row = start if local else shard * size + start
        length = size if part == 0 else half
        if not isinstance(row, int):
            row = pl.multiple_of(row, math.gcd(size, length))
        return ref.at[pl.ds(9 * chunk, 9), pl.ds(row, length)]

    def shard_copy(chunk, k):
        axis, bit, mask, part, source = plan[k]
        there = region(weights, chunk, flipped(mask), part, False)
        src = region(kernel_hbm, chunk, 0, part, False, True) if mask == 0 else there
        device = {"tm": flip(me, bit)} if axis == "tm" else {"groups": 1 - group}
        return copy(src, there, shard_send.at[chunk, k], shard_recv.at[chunk, k], device)

    def shard_arrival(chunk, k):
        axis, bit, mask, part, source = plan[k]
        if axis == "tm":
            here, device = region(weights, chunk, flipped(mask ^ bit), part, False), {"tm": flip(me, bit)}
        else:
            here, device = region(weights, chunk, flipped(mask), part, True), {"groups": 1 - group}
        return copy(here, here, shard_send.at[chunk, k], shard_recv.at[chunk, k], device)

    waited = set()

    def arrive(chunk, k):
        if (chunk, k) in waited:
            return
        waited.add((chunk, k))
        shard_arrival(chunk, k).wait_recv()
        for j, step in enumerate(plan):
            if step[4] == k:
                shard_copy(chunk, j).start()

    early = [k for k, step in enumerate(plan) if step[4] is None and any(s[4] == k for s in plan)]
    later = [k for k, step in enumerate(plan) if step[4] is not None and any(s[4] == k for s in plan)]

    for f in range(frames):
        for direction in (1, -1):

            @pl.when(sends(1, direction))
            def _(f=f, direction=direction):
                line(f, 1, direction).start()

    for chunk in range(CHUNKS):
        for k, step in enumerate(plan):
            if step[4] is None:
                shard_copy(chunk, k).start()
    own_rows = weights.at[:, pl.ds(pl.multiple_of(me * size, size), size)]
    own_copy = pltpu.make_async_copy(kernel_hbm, own_rows, own_sem)
    own_copy.start()

    gain = gain_a[...]
    scale = 1.0 / math.sqrt(channels)
    edges = []

    def edge(number, src, dst, dt, dz):
        t, z = me + dt, tile + dz
        goes = (t < times) & (z >= 0) & (z < tiles)
        comes = (me - dt >= 0) & (tile - dz >= 0) & (tile - dz < tiles)
        move = copy(src, dst, edge_send.at[number], edge_recv.at[number], {"tm": t, "tile": z})

        @pl.when(goes)
        def _():
            move.start()

        edges.append((goes, comes, move, dst))

    for f in range(frames):
        for distance in range(1, tiles):
            for direction in (1, -1):
                comes = tile >= distance if direction > 0 else tile + distance < tiles

                @pl.when(comes)
                def _(f=f, distance=distance, direction=direction):
                    slot = distance if direction > 0 else tiles - distance
                    here = others.at[f, slot - 1]
                    side = 0 if direction > 0 else 1
                    copy(
                        here, here, line_send.at[f, side, distance - 1], line_recv.at[f, slot - 1],
                        {"tile": tile - direction},
                    ).wait_recv()

                if distance + 1 < tiles:

                    @pl.when(sends(distance + 1, direction))
                    def _(f=f, distance=distance, direction=direction):
                        line(f, distance + 1, direction).start()

        if f < CHUNKS and f < frames - 1:
            for k in early:
                arrive(f, k)
        x = act[f]
        normed = split(rms(x, gain))
        queries = dot3(normed, split(wq[...]))
        folded = split(dot3(split(queries), split(wk[...]), TRANSPOSED))
        cells = [normed] + [split(rms(others[f, s], gain)) for s in range(tiles - 1)]
        keys = tuple(jnp.concatenate([c[i] for c in cells], axis=0) for i in range(2))
        scores = dot3(folded, keys, TRANSPOSED) * scale
        powers = jnp.exp(scores - jnp.max(scores, axis=-1, keepdims=True))
        summed = jnp.sum(powers, axis=-1, keepdims=True)
        gathered = dot3(split(powers), keys) / summed
        mixed = dot3(split(gathered), split(wv[...]))
        result = x + dot3(split(mixed), split(wo[...]))
        attended[f] = result
        v = rms(result, gain_c[...])
        hid[f] = (v / (1.0 + jnp.exp(-v))).reshape(rows, width, channels)
        base = 5 * f
        edge(base, hid.at[f, rows - 1], up.at[f], 0, 1)
        edge(base + 1, hid.at[f, 0], down.at[f], 0, -1)
        if f >= frames - 2:
            p = f - (frames - 2)
            edge(base + 2, hid.at[f], past.at[p], 1, 0)
            edge(base + 3, hid.at[f, rows - 1], past_up.at[p], 1, 1)
            edge(base + 4, hid.at[f, 0], past_down.at[p], 1, -1)
        if f < CHUNKS and f < frames - 1:
            for k in later:
                arrive(f, k)

    for chunk in range(CHUNKS):
        for k in early:
            arrive(chunk, k)
    for goes, comes, move, dst in edges:

        @pl.when(comes)
        def _(move=move):
            move.wait_recv()

        @pl.when(jnp.logical_not(comes))
        def _(dst=dst):
            dst[...] = jnp.zeros(dst.shape, F32)

    cell = lax.broadcasted_iota(jnp.int32, (width, channels), 0)
    for f in range(frames + 2):
        for r in range(rows + 2):
            upper, middle, lower, t = (past_up, past, past_down, f) if f < 2 else (up, hid, down, f - 2)
            value = upper[t] if r == 0 else lower[t] if r == rows + 1 else middle[t, r - 1]
            before = jnp.where(cell == 0, 0.0, pltpu.roll(value, 1, 0))
            after = jnp.where(cell == width - 1, 0.0, pltpu.roll(value, width - 1, 0))
            for c, v in enumerate((before, value, after)):
                high, low = split(v)
                xh[f, r, :, c * channels : (c + 1) * channels] = high
                xl[f, r, :, c * channels : (c + 1) * channels] = low
    for chunk in range(CHUNKS):
        for k in later:
            arrive(chunk, k)
    own_copy.wait()
    pixels = frames * tokens
    for a in range(CHUNKS):
        for k in range(len(plan)):
            arrive(a, k)

        def row_taps(b, carry, a=a):
            block = weights[pl.ds(9 * a + 3 * b, 3)].reshape(3 * channels, channels)
            high = xh[pl.ds(a, frames), pl.ds(b, rows)].reshape(pixels, 3 * channels)
            low = xl[pl.ds(a, frames), pl.ds(b, rows)].reshape(pixels, 3 * channels)
            product = dot3((high, low), split(block))
            out[...] = out[...] + product
            return carry

        if a == 0:
            out[...] = jnp.zeros(out.shape, F32)
        lax.fori_loop(0, 3, row_taps, 0)

    for f in range(frames):
        for distance in range(1, tiles):
            for direction in (1, -1):

                @pl.when(sends(distance, direction))
                def _(f=f, distance=distance, direction=direction):
                    line(f, distance, direction).wait_send()

    for goes, comes, move, dst in edges:

        @pl.when(goes)
        def _(move=move):
            move.wait_send()

    for chunk in range(CHUNKS):
        for k in range(len(plan)):
            shard_copy(chunk, k).wait_send()


def body(activations, gain_attention, w_query, w_key, w_value, w_out, gain_conv, conv_weight):
    frames, rows, width, channels = activations.shape
    tokens = rows * width
    own = activations.reshape(frames, tokens, channels)
    times, tiles = lax.axis_size("tm"), lax.axis_size("tile")
    taps, size = conv_weight.shape[:2]
    plan = shard_plan(times, lax.axis_size("groups") == 2 and size % 16 == 0)
    vmem = pl.BlockSpec(memory_space=pltpu.VMEM)
    dma = pltpu.SemaphoreType.DMA
    attended, conv_out = pl.pallas_call(
        functools.partial(kernel, plan, times, tiles),
        in_specs=[vmem] * 7 + [pl.BlockSpec(memory_space=pl.ANY)],
        out_specs=[vmem, vmem],
        out_shape=[
            jax.ShapeDtypeStruct(own.shape, F32),
            jax.ShapeDtypeStruct((frames * tokens, channels), F32),
        ],
        scratch_shapes=[
            pltpu.VMEM((frames, tiles - 1, tokens, channels), F32),
            pltpu.VMEM((frames, rows, width, channels), F32),
            pltpu.VMEM((frames, width, channels), F32),
            pltpu.VMEM((frames, width, channels), F32),
            pltpu.VMEM((2, rows, width, channels), F32),
            pltpu.VMEM((2, width, channels), F32),
            pltpu.VMEM((2, width, channels), F32),
            pltpu.VMEM((taps, channels, channels), F32),
            pltpu.VMEM((frames + 2, rows + 2, width, 3 * channels), BF16),
            pltpu.VMEM((frames + 2, rows + 2, width, 3 * channels), BF16),
            dma((frames, 2, tiles - 1)),
            dma((frames, tiles - 1)),
            dma((5 * frames,)),
            dma((5 * frames,)),
            dma((CHUNKS, len(plan))),
            dma((CHUNKS, len(plan))),
            dma,
        ],
        compiler_params=pltpu.CompilerParams(
            collective_id=0, has_side_effects=True, vmem_limit_bytes=VMEM_LIMIT
        ),
    )(
        own, gain_attention.reshape(1, -1), w_query, w_key, w_value, w_out, gain_conv.reshape(1, -1), conv_weight
    )
    return (attended.reshape(activations.shape), conv_out.reshape(activations.shape))


def solution(mesh):
    placed = P(("groups", "tm"), "tile", None, None)
    return jax.shard_map(
        body,
        mesh=mesh,
        in_specs=(placed, P(), P(), P(), P(), P(), P(), P(None, "tm", None)),
        out_specs=(placed, placed),
        check_vma=False,
    )
```

```python
import functools
import math

import jax
import jax.numpy as jnp
from jax import lax
from jax.experimental import pallas as pl
from jax.experimental.pallas import tpu as pltpu
from jax.sharding import PartitionSpec as P

F32, BF16 = jnp.float32, jnp.bfloat16
VMEM_LIMIT = 56 * 1024 * 1024
CHUNKS = 3


def split(x):
    high = x.astype(BF16)
    return high, (x - high.astype(F32)).astype(BF16)


def dot3(a, b, dims=(((1,), (0,)), ((), ()))):
    dot = functools.partial(lax.dot_general, dimension_numbers=dims, preferred_element_type=F32)
    (ah, al), (bh, bl) = a, b
    return dot(ah, bh) + (dot(ah, bl) + dot(al, bh))


TRANSPOSED = (((1,), (1,)), ((), ()))


def rms(v, gain):
    return v * lax.rsqrt(jnp.mean(v * v, axis=-1, keepdims=True) + 1e-06) * gain


MESH = pl.DeviceIdType.MESH


def shard_plan(shards, halved):
    plan, held = [], [(0, 0, None)]
    bit = 1
    while 2 * bit < shards:
        bit *= 2
    while bit >= 1 and shards > 1:
        arrived = []
        for mask, part, source in held:
            if halved and bit > 1 and part == 0:
                plan.append(("tm", bit, mask, 1, source))
                plan.append(("groups", 1, mask ^ bit, 1, len(plan) - 1))
                arrived += [(mask ^ bit, 1, len(plan) - 2), (mask ^ bit, 2, len(plan) - 1)]
            else:
                plan.append(("tm", bit, mask, part, source))
                arrived.append((mask ^ bit, part, len(plan) - 1))
        held += arrived
        bit //= 2
    return plan


def kernel(
    plan, times, tiles, act, gain_a, wq, wk, wv, wo, gain_c, kernel_hbm, attended, out,
    others, hid, up, down, past, past_up, past_down, weights, xh, xl,
    line_send, line_recv, edge_send, edge_recv, shard_send, shard_recv, own_sem,
):
    frames, rows, width, channels = hid.shape
    tokens = rows * width
    group, me, tile = lax.axis_index("groups"), lax.axis_index("tm"), lax.axis_index("tile")
    size = kernel_hbm.shape[1]
    half = size // 2

    barrier = pltpu.get_barrier_semaphore()
    friends = [(True, {"groups": 1 - group})]
    bit = 1
    while bit < times:
        friends.append((True, {"tm": me + bit * (1 - 2 * ((me // bit) % 2))}))
        bit *= 2
    for dt, dz in ((0, 1), (1, 0), (1, 1), (1, -1)):
        for sign in (1, -1):
            t, z = me + sign * dt, tile + sign * dz
            inside = (t >= 0) & (t < times) & (z >= 0) & (z < tiles)
            friends.append((inside, {"tm": t, "tile": z}))
    count = 0
    for inside, device in friends:
        if inside is True:
            pl.semaphore_signal(barrier, inc=1, device_id=device, device_id_type=MESH)
            count = count + 1
        else:

            @pl.when(inside)
            def _(device=device):
                pl.semaphore_signal(barrier, inc=1, device_id=device, device_id_type=MESH)

            count = count + inside.astype(jnp.int32)
    pl.semaphore_wait(barrier, count)

    def copy(src, dst, send, recv, device):
        return pltpu.make_async_remote_copy(
            src_ref=src, dst_ref=dst, send_sem=send, recv_sem=recv, device_id=device, device_id_type=MESH
        )

    def line(f, distance, direction):
        slot_here = distance - 1 if direction > 0 else tiles - distance + 1
        slot_there = distance if direction > 0 else tiles - distance
        src = act.at[f] if distance == 1 else others.at[f, slot_here - 1]
        side = 0 if direction > 0 else 1
        return copy(
            src, others.at[f, slot_there - 1], line_send.at[f, side, distance - 1],
            line_recv.at[f, slot_there - 1], {"tile": tile + direction},
        )

    def sends(distance, direction):
        if direction > 0:
            return (tile >= distance - 1) & (tile < tiles - 1)
        return (tile + distance - 1 <= tiles - 1) & (tile > 0)

    def flip(value, bit):
        return value + bit * (1 - 2 * ((value // bit) % 2))

    def flipped(mask):
        value, bit = me, 1
        while bit <= mask:
            if mask & bit:
                value = flip(value, bit)
            bit *= 2
        return value

    def region(ref, chunk, shard, part, swap, local=False):
        first = group if not swap else 1 - group
        start = {0: 0, 1: first * half, 2: (1 - first) * half}[part]
        row = start if local else shard * size + start
        length = size if part == 0 else half
        if not isinstance(row, int):
            row = pl.multiple_of(row, math.gcd(size, length))
        return ref.at[pl.ds(9 * chunk, 9), pl.ds(row, length)]

    def shard_copy(chunk, k):
        axis, bit, mask, part, source = plan[k]
        there = region(weights, chunk, flipped(mask), part, False)
        src = region(kernel_hbm, chunk, 0, part, False, True) if mask == 0 else there
        device = {"tm": flip(me, bit)} if axis == "tm" else {"groups": 1 - group}
        return copy(src, there, shard_send.at[chunk, k], shard_recv.at[chunk, k], device)

    def shard_arrival(chunk, k):
        axis, bit, mask, part, source = plan[k]
        if axis == "tm":
            here, device = region(weights, chunk, flipped(mask ^ bit), part, False), {"tm": flip(me, bit)}
        else:
            here, device = region(weights, chunk, flipped(mask), part, True), {"groups": 1 - group}
        return copy(here, here, shard_send.at[chunk, k], shard_recv.at[chunk, k], device)

    early = [k for k, step in enumerate(plan) if step[4] is None and any(s[4] == k for s in plan)]
    later = [k for k, step in enumerate(plan) if step[4] is not None and any(s[4] == k for s in plan)]

    waited = set()

    def arrive(chunk, k):
        if (chunk, k) in waited:
            return
        waited.add((chunk, k))
        shard_arrival(chunk, k).wait_recv()
        if k in early and chunk + 1 < CHUNKS:
            shard_copy(chunk + 1, k).start()
        for j, step in enumerate(plan):
            if step[4] == k:
                shard_copy(chunk, j).start()

    def start_line(f):
        for direction in (1, -1):

            @pl.when(sends(1, direction))
            def _(direction=direction):
                line(f, 1, direction).start()

    start_line(0)
    for chunk in range(CHUNKS):
        for k, step in enumerate(plan):
            if step[4] is None and (chunk == 0 or k not in early):
                shard_copy(chunk, k).start()
    own_rows = weights.at[:, pl.ds(pl.multiple_of(me * size, size), size)]
    own_copy = pltpu.make_async_copy(kernel_hbm, own_rows, own_sem)
    own_copy.start()

    cell = lax.broadcasted_iota(jnp.int32, (width, channels), 0)

    def place(f, r):
        upper, middle, lower, t = (past_up, past, past_down, f) if f < 2 else (up, hid, down, f - 2)
        value = upper[t] if r == 0 else lower[t] if r == rows + 1 else middle[t, r - 1]
        before = jnp.where(cell == 0, 0.0, pltpu.roll(value, 1, 0))
        after = jnp.where(cell == width - 1, 0.0, pltpu.roll(value, width - 1, 0))
        for c, v in enumerate((before, value, after)):
            high, low = split(v)
            xh[f, r, :, c * channels : (c + 1) * channels] = high
            xl[f, r, :, c * channels : (c + 1) * channels] = low

    gain = gain_a[...].reshape(1, channels)
    scale = 1.0 / math.sqrt(channels)
    edges = []

    def edge(number, src, dst, dt, dz):
        t, z = me + dt, tile + dz
        goes = (t < times) & (z >= 0) & (z < tiles)
        comes = (me - dt >= 0) & (tile - dz >= 0) & (tile - dz < tiles)
        move = copy(src, dst, edge_send.at[number], edge_recv.at[number], {"tm": t, "tile": z})

        @pl.when(goes)
        def _():
            move.start()

        edges.append((goes, comes, move, dst))

    for f in range(frames):
        for distance in range(1, tiles):
            for direction in (1, -1):
                comes = tile >= distance if direction > 0 else tile + distance < tiles

                @pl.when(comes)
                def _(f=f, distance=distance, direction=direction):
                    slot = distance if direction > 0 else tiles - distance
                    here = others.at[f, slot - 1]
                    side = 0 if direction > 0 else 1
                    copy(
                        here, here, line_send.at[f, side, distance - 1], line_recv.at[f, slot - 1],
                        {"tile": tile - direction},
                    ).wait_recv()

                if distance + 1 < tiles:

                    @pl.when(sends(distance + 1, direction))
                    def _(f=f, distance=distance, direction=direction):
                        line(f, distance + 1, direction).start()

            if distance == 1 and f + 1 < frames:
                start_line(f + 1)
        if tiles == 1 and f + 1 < frames:
            start_line(f + 1)
        if f < CHUNKS and f < frames - 1:
            for k in early:
                arrive(f, k)
        x = act[f]
        normed = split(rms(x, gain))
        queries = dot3(normed, split(wq[...]))
        folded = split(dot3(split(queries), split(wk[...]), TRANSPOSED))
        cells = [normed] + [split(rms(others[f, s], gain)) for s in range(tiles - 1)]
        keys = tuple(jnp.concatenate([c[i] for c in cells], axis=0) for i in range(2))
        scores = dot3(folded, keys, TRANSPOSED) * scale
        powers = jnp.exp(scores - jnp.max(scores, axis=-1, keepdims=True))
        summed = jnp.sum(powers, axis=-1, keepdims=True)
        gathered = dot3(split(powers), keys) / summed
        mixed = dot3(split(gathered), split(wv[...]))
        result = x + dot3(split(mixed), split(wo[...]))
        attended[f] = result
        v = rms(result, gain_c[...].reshape(1, channels))
        hid[f] = (v / (1.0 + jnp.exp(-v))).reshape(rows, width, channels)
        base = 5 * f
        edge(base, hid.at[f, rows - 1], up.at[f], 0, 1)
        edge(base + 1, hid.at[f, 0], down.at[f], 0, -1)
        if f >= frames - 2:
            p = f - (frames - 2)
            edge(base + 2, hid.at[f], past.at[p], 1, 0)
            edge(base + 3, hid.at[f, rows - 1], past_up.at[p], 1, 1)
            edge(base + 4, hid.at[f, 0], past_down.at[p], 1, -1)
        for r in range(1, rows + 1):
            place(f + 2, r)
        if 1 <= f < frames - 1 and f <= CHUNKS:
            for k in later:
                arrive(f - 1, k)

    for chunk in range(CHUNKS):
        for k in early:
            arrive(chunk, k)
    for goes, comes, move, dst in edges:

        @pl.when(comes)
        def _(move=move):
            move.wait_recv()

        @pl.when(jnp.logical_not(comes))
        def _(dst=dst):
            dst[...] = jnp.zeros(dst.shape, F32)

    for f in range(frames + 2):
        for r in range(rows + 2):
            if f < 2 or r in (0, rows + 1):
                place(f, r)
    for chunk in range(CHUNKS):
        for k in later:
            arrive(chunk, k)
    own_copy.wait()
    pixels = frames * tokens
    for a in range(CHUNKS):
        for k in range(len(plan)):
            arrive(a, k)

        def row_taps(b, carry, a=a):
            block = weights[pl.ds(9 * a + 3 * b, 3)].reshape(3 * channels, channels)
            high = xh[pl.ds(a, frames), pl.ds(b, rows)].reshape(pixels, 3 * channels)
            low = xl[pl.ds(a, frames), pl.ds(b, rows)].reshape(pixels, 3 * channels)
            product = dot3((high, low), split(block))
            out[...] = out[...] + product
            return carry

        if a == 0:
            out[...] = jnp.zeros(out.shape, F32)
        lax.fori_loop(0, 3, row_taps, 0)

    for f in range(frames):
        for distance in range(1, tiles):
            for direction in (1, -1):

                @pl.when(sends(distance, direction))
                def _(f=f, distance=distance, direction=direction):
                    line(f, distance, direction).wait_send()

    for goes, comes, move, dst in edges:

        @pl.when(goes)
        def _(move=move):
            move.wait_send()

    for chunk in range(CHUNKS):
        for k in range(len(plan)):
            shard_copy(chunk, k).wait_send()


def body(activations, gain_attention, w_query, w_key, w_value, w_out, gain_conv, conv_weight):
    frames, rows, width, channels = activations.shape
    tokens = rows * width
    own = activations.reshape(frames, tokens, channels)
    times, tiles = lax.axis_size("tm"), lax.axis_size("tile")
    taps, size = conv_weight.shape[:2]
    plan = shard_plan(times, lax.axis_size("groups") == 2 and size % 16 == 0)
    vmem = pl.BlockSpec(memory_space=pltpu.VMEM)
    dma = pltpu.SemaphoreType.DMA
    attended, conv_out = pl.pallas_call(
        functools.partial(kernel, plan, times, tiles),
        in_specs=[vmem] * 7 + [pl.BlockSpec(memory_space=pl.ANY)],
        out_specs=[vmem, vmem],
        out_shape=[
            jax.ShapeDtypeStruct(own.shape, F32),
            jax.ShapeDtypeStruct((frames * tokens, channels), F32),
        ],
        scratch_shapes=[
            pltpu.VMEM((frames, tiles - 1, tokens, channels), F32),
            pltpu.VMEM((frames, rows, width, channels), F32),
            pltpu.VMEM((frames, width, channels), F32),
            pltpu.VMEM((frames, width, channels), F32),
            pltpu.VMEM((2, rows, width, channels), F32),
            pltpu.VMEM((2, width, channels), F32),
            pltpu.VMEM((2, width, channels), F32),
            pltpu.VMEM((taps, channels, channels), F32),
            pltpu.VMEM((frames + 2, rows + 2, width, 3 * channels), BF16),
            pltpu.VMEM((frames + 2, rows + 2, width, 3 * channels), BF16),
            dma((frames, 2, tiles - 1)),
            dma((frames, tiles - 1)),
            dma((5 * frames,)),
            dma((5 * frames,)),
            dma((CHUNKS, len(plan))),
            dma((CHUNKS, len(plan))),
            dma,
        ],
        compiler_params=pltpu.CompilerParams(
            collective_id=0, has_side_effects=True, vmem_limit_bytes=VMEM_LIMIT
        ),
    )(
        own, gain_attention, w_query, w_key, w_value, w_out, gain_conv, conv_weight
    )
    return (attended.reshape(activations.shape), conv_out.reshape(activations.shape))


def solution(mesh):
    placed = P(("groups", "tm"), "tile", None, None)
    return jax.shard_map(
        body,
        mesh=mesh,
        in_specs=(placed, P(), P(), P(), P(), P(), P(), P(None, "tm", None)),
        out_specs=(placed, placed),
        check_vma=False,
    )
```
